32 devices in a mesh: grp: 2 (over x), gy: 16 (over z, y, core).
Axes of the slice: x: 2, y: 2, z: 4, core: 2. Of those that a mesh axis runs over, the one named last changes fastest.
Arguments:
- vectors: bfloat16 [512, 2, 3, 16, 512], P('grp', None, None, 'gy'), parts along dimension 0, may hold values from -6 to 6
- gauge_links: bfloat16 [4, 2, 3, 3, 16, 512], P('grp', None, None, None, 'gy'), parts along dimension 0, may hold values from -4 to 4
- perambulators: bfloat16 [32, 4, 2, 2, 256, 256], P('grp', None, None, None, 'gy'), parts along dimension 0, may hold values from -0.25 to 0.25
- momenta: int32 [4, 3], replicated, may hold values from -2 to 2
- path_codes: int32 [2, 2], replicated, may hold values from 0 to 1
- source_times: int32 [8], P('grp'), parts along dimension 0, may hold values from 0 to 15
Outputs:
- contracted: bfloat16 [8, 4, 2, 256, 2, 4, 2, 256], P('grp', None, None, 'gy'), parts along dimension 0
The draws below stay inside these ranges and needn't reach their ends.
There are 2 independent parts, one for each index of `grp`. The reference program is written for one: setup_inputs(seed, part) draws one part's arguments, and reference() takes and returns one part's arrays. A program takes and returns all parts, laid end to end along the dimension named above; an argument that names none is the same for every part. Nothing has to cross between parts.
Inputs may be any that keep to these rules, and one draw needn't show every extreme that they name: `momenta`: momentum components in lattice units.
All inputs are finite; a program needn't handle non-finite values.
Results may differ from the reference program's by a relative error of at most 0.0057.
Values may be sent and summed in bfloat16 or wider, within the bound.
No kernel may reach another device: no remote copies, remote signals or barrier semaphores. Data moves between devices by JAX's collectives and lax.ppermute only.
A program may use at most 128 MiB of HBM per device.

```python
import math
import jax
import jax.numpy as jnp
from jax import lax

NVEC = 256
LX = 32
LZ = 16
NMOM = 4
NDISP = 2
NT0 = 16
NSRC = 4
NY = 16
ZX = 512


def set_ends(result, rng, least, top_value):
    longest = result.shape.index(max(result.shape))
    spots = []
    for shift in (0, 1):
        where = [jax.random.randint(jax.random.fold_in(rng, axis), (), 0, length) for axis, length in enumerate(result.shape)]
        where[longest] = (where[longest] + shift) % result.shape[longest]
        spots.append(tuple(where))
    return result.at[spots[0]].set(least).at[spots[1]].set(top_value)


def spiked(drawn, own_key, source, target, blocks, factor):
    owner, partner = [(jnp.arange(drawn.shape[dim]) // (drawn.shape[dim] // blocks)).reshape([-1 if axis == dim else 1 for axis in range(drawn.ndim)]) for dim in (source, target)]
    chosen = jax.random.permutation(own_key, blocks)[partner]
    strong = (owner == chosen) | (owner == (partner + blocks // 2) % blocks)
    return jnp.where(strong, factor * drawn, drawn)


def block_scale(stream_key, extent, shards, low, top_value):
    def one(axis_at, shards_of):
        draws = jax.random.uniform(jax.random.fold_in(jax.random.fold_in(stream_key, 6), axis_at), (shards_of,), jnp.float32, low / len(shards), top_value / len(shards))
        return jnp.repeat(jnp.exp(draws), extent[axis_at] // shards_of).reshape((-1,) + (1,) * (len(extent) - axis_at - 1))

    loudness = one(*shards[0])
    for cut in shards[1:]:
        loudness = loudness * one(*cut)
    return loudness


def gaussian(key, dims, spread, bound, cuts=(), kind=jnp.bfloat16):
    gain = block_scale(key, dims, cuts, -0.22, 0.18) if cuts else 1.0
    drawn = jax.random.normal(key, dims, jnp.float32) * spread * gain
    return jnp.minimum(jnp.maximum(drawn, -bound), bound).astype(kind)


def bell_draw_with(stream_key, shape, deviation, limit, shards, heavy, kind=jnp.bfloat16):
    array = deviation * jax.random.normal(stream_key, shape, jnp.float32)
    if shards:
        array = array * block_scale(stream_key, shape, shards, -0.22, 0.18)
    return jnp.clip(spiked(array, jax.random.fold_in(stream_key, 3), *heavy), -limit, limit).astype(kind)


def setup_inputs(seed: int = 0, part: int = 0) -> dict:
    streams_of = jax.random.split(jax.random.key(seed), 7)
    part_splits = jax.random.split(jax.random.fold_in(streams_of[6], part), 7)
    return {
        "vectors": bell_draw_with(part_splits[0], (NVEC, 2, 3, NY, ZX), 1.0, 6.0, ((3, 16),), (3, 0, 16, 2.0)),
        "gauge_links": gaussian(part_splits[1], (2, 2, 3, 3, NY, ZX), 0.577, 4.0, ((4, 16),)),
        "perambulators": gaussian(part_splits[2], (NT0, 4, 2, 2, NVEC, NVEC), (2 * NVEC) ** -0.5, 0.25, ((4, 16),)),
        "momenta": set_ends(jax.random.randint(streams_of[3], (NMOM, 3), -2, 3), jax.random.fold_in(streams_of[3], 1), -2, 2).astype(jnp.int32),
        "path_codes": set_ends(jax.random.randint(streams_of[4], (NDISP, 2), 0, 2), jax.random.fold_in(streams_of[4], 1), 0, 1).astype(jnp.int32),
        "source_times": set_ends(jax.random.randint(part_splits[5], (NSRC,), 0, NT0), jax.random.fold_in(part_splits[5], 1), 0, NT0 - 1).astype(jnp.int32),
    }


TWO_PI = 6.283185307179586
HIGHEST = lax.Precision.HIGHEST

def color_apply(link_re, link_im, source_re, source_im, dagger):
    if dagger:
        link_re = jnp.swapaxes(link_re, 0, 1)
        link_im = -jnp.swapaxes(link_im, 0, 1)
    real_part = link_re[:, 0][None] * source_re[:, 0][:, None] - link_im[:, 0][None] * source_im[:, 0][:, None]
    imag_part = link_re[:, 0][None] * source_im[:, 0][:, None] + link_im[:, 0][None] * source_re[:, 0][:, None]
    for column in range(1, 3):
        real_part = real_part + link_re[:, column][None] * source_re[:, column][:, None] - link_im[:, column][None] * source_im[:, column][:, None]
        imag_part = imag_part + link_re[:, column][None] * source_im[:, column][:, None] + link_im[:, column][None] * source_re[:, column][:, None]
    return jnp.stack([real_part, imag_part], axis=1)

def link_step(link_data, source_field, dagger):
    return color_apply(link_data[0].astype(jnp.float32), link_data[1].astype(jnp.float32), source_field[:, 0].astype(jnp.float32), source_field[:, 1].astype(jnp.float32), dagger)

def z_step(links_z, source_field, code_value):

    def ahead(field):
        return color_apply(links_z[0], links_z[1], jnp.roll(field[:, 0], -LX, -1), jnp.roll(field[:, 1], -LX, -1), False)

    def behind(field):
        return color_apply(jnp.roll(links_z[0], LX, -1), jnp.roll(links_z[1], LX, -1), jnp.roll(field[:, 0], LX, -1), jnp.roll(field[:, 1], LX, -1), True)
    return lax.cond(code_value == 1, ahead, behind, source_field)

def phase_angles(momenta, y_coord, y_total):
    positions = jnp.arange(LZ * LX, dtype=jnp.int32)
    x_coord = positions % LX
    z_coord = positions // LX
    mom_x = momenta[:, 0][:, None, None]
    mom_y = momenta[:, 1][:, None, None]
    mom_z = momenta[:, 2][:, None, None]
    period = LX * y_total * LZ
    raw_phase = mom_x * x_coord[None, None, :] * (y_total * LZ) + mom_y * y_coord[None, :, None] * (LX * LZ) + mom_z * z_coord[None, None, :] * (LX * y_total)
    residue = jnp.mod(raw_phase, period)
    return residue.astype(jnp.float32) * (TWO_PI / period)

def phased_rows(source_field, angles):
    cosine = jnp.cos(angles)[:, None, None]
    sine_part = jnp.sin(angles)[:, None, None]
    real_in = source_field[None, :, 0]
    imag_in = source_field[None, :, 1]
    stacked = jnp.stack([cosine * real_in + sine_part * imag_in, cosine * imag_in - sine_part * real_in], axis=2)
    return stacked.astype(jnp.bfloat16).reshape(angles.shape[0] * source_field.shape[0], -1)

def conj_rows(vectors):
    vec_count = vectors.shape[0]
    plain_rows = vectors.reshape(vec_count, -1)
    swapped = jnp.concatenate([-vectors[:, 1], vectors[:, 0]], axis=1).reshape(vec_count, -1)
    return jnp.concatenate([plain_rows, swapped], axis=0)

def reference(vectors, gauge_links, perambulators, momenta, path_codes, source_times):
    links_y = gauge_links[0]
    links_z = gauge_links[1].astype(jnp.float32)

    def y_ahead(field):
        return link_step(links_y, jnp.roll(field, -1, axis=3), False)

    def y_behind(field):
        return link_step(jnp.roll(links_y, 1, axis=3), jnp.roll(field, 1, axis=3), True)
    angles = phase_angles(momenta, jnp.arange(NY, dtype=jnp.int32), NY)
    left_rows = conj_rows(vectors).astype(jnp.float32)
    norm_factor = 1.0 / math.sqrt(6 * NY * ZX)
    elementals = []
    for path_index in range(NDISP):
        shifted = lax.cond(path_codes[path_index, 0] == 1, y_ahead, y_behind, vectors)
        shifted = z_step(links_z, shifted, path_codes[path_index, 1])
        right_rows = phased_rows(shifted, angles).astype(jnp.float32)
        partial_value = jnp.dot(left_rows, right_rows.T, precision=HIGHEST)
        elementals.append((partial_value * norm_factor).astype(jnp.bfloat16).reshape(2, NVEC, NMOM, NVEC))
    elemental = jnp.stack(elementals).astype(jnp.float32)
    chosen = perambulators[source_times].astype(jnp.float32)
    pattern = 'sabik,pkmj->sabipmj'
    chosen_re = chosen[:, :, :, 0]
    chosen_im = chosen[:, :, :, 1]
    first = jnp.einsum(pattern, chosen_re, elemental[:, 0], precision=HIGHEST) - jnp.einsum(pattern, chosen_im, elemental[:, 1], precision=HIGHEST)
    second = jnp.einsum(pattern, chosen_re, elemental[:, 1], precision=HIGHEST) + jnp.einsum(pattern, chosen_im, elemental[:, 0], precision=HIGHEST)
    return jnp.stack([first, second], axis=6).astype(jnp.bfloat16)
```

```python
import functools
import math

import jax
import jax.numpy as jnp
from jax import lax
from jax.experimental import pallas as pl
from jax.experimental.pallas import tpu as pltpu
from jax.sharding import PartitionSpec as P

LX = 32
LZ = 16
LANES = 128
ROWS = 16
TWO_PI = 6.283185307179586

F32 = jnp.float32
BF16 = jnp.bfloat16
NT = (((1,), (1,)), ((), ()))


def complex_product(left, right):
    left_re, left_im = left[0][:, :, None], left[1][:, :, None]
    right_re, right_im = right[0][None], right[1][None]
    real_part = (left_re * right_re - left_im * right_im).sum(1)
    imag_part = (left_re * right_im + left_im * right_re).sum(1)
    return jnp.stack([real_part, imag_part])


def adjoint(link):
    return jnp.stack([jnp.swapaxes(link[0], 0, 1), -jnp.swapaxes(link[1], 0, 1)])


def path_tables(link_y, link_z, link_z_next, momenta, code, y_coord, y_total):
    site_count = link_y.shape[-1]
    ahead_y, ahead_z = code[0] == 1, code[1] == 1
    step_y = jnp.where(ahead_y, link_y, adjoint(link_y))
    z_plane = jnp.where(ahead_y, link_z, link_z_next)
    step_z = jnp.where(ahead_z, jnp.roll(z_plane, LX, -1), adjoint(z_plane))
    matrix = complex_product(step_z, step_y).reshape(18, site_count)
    positions = jnp.arange(site_count, dtype=jnp.int32)
    positions = jnp.mod(jnp.where(ahead_z, positions - LX, positions + LX), site_count)
    y_here = jnp.mod(jnp.where(ahead_y, y_coord, y_coord + 1), y_total)
    period = LX * y_total * LZ
    raw_phase = (
        momenta[:, 0:1] * (positions % LX)[None] * (y_total * LZ)
        + momenta[:, 1:2] * y_here * (LX * LZ)
        + momenta[:, 2:3] * (positions // LX)[None] * (LX * y_total)
    )
    angles = jnp.mod(raw_phase, period).astype(F32) * (TWO_PI / period)
    return jnp.concatenate([matrix, jnp.cos(angles), jnp.sin(angles)], axis=0)


def build_left(source, shift, left):
    planes, count, sites = source.shape
    half = planes // 2
    for plane in range(planes):
        field = source[plane]
        field = jnp.concatenate([field[:, sites - shift :], field[:, : sites - shift]], axis=1)
        left[:count, plane * sites : (plane + 1) * sites] = field
        if plane < half:
            other = (plane + half) * sites
            left[count:, other : other + sites] = field
        if plane >= half:
            other = (plane - half) * sites
            left[count:, other : other + sites] = -field


def build_right(source, table, right, mom_count):
    planes, count, sites = source.shape
    for lane in range(0, sites, LANES):
        cols = slice(lane, lane + LANES)
        rows = [
            jnp.broadcast_to(table[k : k + 1, cols], (ROWS, LANES))
            for k in range(18 + 2 * mom_count)
        ]

        def step(group, carry):
            start = pl.multiple_of(group * ROWS, ROWS)
            field = [source[plane, pl.ds(start, ROWS), cols].astype(F32) for plane in range(6)]
            for out in range(3):
                real_part = imag_part = None
                for col in range(3):
                    m_re, m_im = rows[out * 3 + col], rows[9 + out * 3 + col]
                    v_re, v_im = field[col], field[3 + col]
                    term_re = m_re * v_re - m_im * v_im
                    term_im = m_re * v_im + m_im * v_re
                    real_part = term_re if real_part is None else real_part + term_re
                    imag_part = term_im if imag_part is None else imag_part + term_im
                for mom in range(mom_count):
                    cosine, sine = rows[18 + mom], rows[18 + mom_count + mom]
                    dest = pl.ds(pl.multiple_of(mom * count + start, ROWS), ROWS)
                    right[dest, out * sites + lane : out * sites + lane + LANES] = (
                        cosine * real_part + sine * imag_part
                    ).astype(BF16)
                    right[dest, (3 + out) * sites + lane : (3 + out) * sites + lane + LANES] = (
                        cosine * imag_part - sine * real_part
                    ).astype(BF16)
            return carry

        lax.fori_loop(0, count // ROWS, step, 0)


def elemental_kernel(mom_count, code, here, after, table, out, left, right):
    count, sites = here.shape[1], here.shape[2]

    for ahead_y in (0, 1):
        left_source, right_source = (here, after) if ahead_y else (after, here)

        @pl.when((code[0] == 1) == bool(ahead_y))
        def _():
            for ahead_z in (0, 1):

                @pl.when((code[1] == 1) == bool(ahead_z))
                def _():
                    build_left(left_source, LX if ahead_z else sites - LX, left)

            build_right(right_source, table, right, mom_count)

    for mom in range(mom_count):
        product = lax.dot_general(
            left[...], right[mom * count : (mom + 1) * count], NT, preferred_element_type=F32
        )
        out[:, mom * count : (mom + 1) * count] = product[:count]
        other = (mom_count + mom) * count
        out[:, other : other + count] = product[count:]


def partial_elemental(code, here, after, table, mom_count):
    planes, count, sites = here.shape
    flops = 2 * 2 * count * planes * sites * mom_count * count
    return pl.pallas_call(
        functools.partial(elemental_kernel, mom_count),
        out_shape=jax.ShapeDtypeStruct((count, 2 * mom_count * count), F32),
        in_specs=[pl.BlockSpec(memory_space=pltpu.SMEM)]
        + [pl.BlockSpec(memory_space=pltpu.VMEM)] * 3,
        out_specs=pl.BlockSpec(memory_space=pltpu.VMEM),
        scratch_shapes=[
            pltpu.VMEM((2 * count, planes * sites), BF16),
            pltpu.VMEM((mom_count * count, planes * sites), BF16),
        ],
        cost_estimate=pl.CostEstimate(flops=flops, bytes_accessed=6 << 20, transcendentals=0),
    )(code, here, after, table)


def swap_pairs(count, bit):
    return [(i, i ^ (1 << bit)) for i in range(count)]


def scatter_rows(cells, axis, order):
    me, count = lax.axis_index(axis), lax.axis_size(axis)
    for bit in order:
        half = cells.shape[0] // 2
        mine = (me >> bit) & 1
        sent = lax.dynamic_slice_in_dim(cells, (1 - mine) * half, half, 0).astype(BF16)
        kept = lax.dynamic_slice_in_dim(cells, mine * half, half, 0)
        cells = kept + lax.ppermute(sent, axis, swap_pairs(count, bit)).astype(F32)
    return cells


def gather_rows(cells, axis, order):
    me, count = lax.axis_index(axis), lax.axis_size(axis)
    for bit in reversed(order):
        other = lax.ppermute(cells, axis, swap_pairs(count, bit))
        upper = ((me >> bit) & 1) == 1
        cells = jnp.concatenate(
            [jnp.where(upper, other, cells), jnp.where(upper, cells, other)], axis=0
        )
    return cells


def contract_kernel(path, left, block, *refs):
    out, tiles, sems = refs[-3:]
    row_count, mom_count, width = out.shape[0], out.shape[2], out.shape[4]
    count = block.shape[0]
    copies = []
    for mom in range(mom_count):
        for lane in range(0, width, LANES):
            col = mom * width + lane
            other = mom_count * width + col
            product = jnp.dot(
                left[:, :count], block[:, col : col + LANES], preferred_element_type=F32
            ) + jnp.dot(
                left[:, count:], block[:, other : other + LANES], preferred_element_type=F32
            )
            slot = len(copies)
            tiles[slot] = product.astype(BF16).reshape(row_count, 2, LANES)
            copy = pltpu.make_async_copy(
                tiles.at[slot], out.at[:, path, mom, :, lane : lane + LANES], sems.at[slot]
            )
            copy.start()
            copies.append(copy)
    for copy in copies:
        copy.wait()


def contract(path, left, block, shape, before):
    slots = shape[2] * (shape[4] // LANES)
    operands = [left, block] + ([] if before is None else [before])
    return pl.pallas_call(
        functools.partial(contract_kernel, path),
        out_shape=jax.ShapeDtypeStruct(shape, BF16),
        in_specs=[pl.BlockSpec(memory_space=pltpu.VMEM)] * 2
        + ([] if before is None else [pl.BlockSpec(memory_space=pl.ANY)]),
        out_specs=pl.BlockSpec(memory_space=pl.ANY),
        scratch_shapes=[
            pltpu.VMEM((slots, shape[0], 2, LANES), BF16),
            pltpu.SemaphoreType.DMA((slots,)),
        ],
        input_output_aliases={} if before is None else {2: 0},
        cost_estimate=pl.CostEstimate(
            flops=8 * shape[0] * shape[2] * shape[4] * block.shape[0],
            bytes_accessed=4 << 20,
            transcendentals=0,
        ),
    )(*operands)


def shards(vectors, gauge_links, perambulators, momenta, path_codes, source_times):
    vec_count, _, _, y_rows, site_count = vectors.shape
    y_devices = lax.axis_size("gy")
    y_total = y_rows * y_devices
    mom_count, path_total = momenta.shape[0], path_codes.shape[0]
    bits = y_devices.bit_length() - 1
    down = [((i + 1) % y_devices, i) for i in range(y_devices)]

    first = lax.slice_in_dim(vectors, 0, 1, axis=3)
    incoming = lax.ppermute(first, "gy", down)
    z_links = gauge_links[1].astype(F32)
    z_incoming = lax.ppermute(gauge_links[1][:, :, :, :1], "gy", down).astype(F32)

    def planes_of(field):
        return field.reshape(vec_count, 6, site_count).transpose(1, 0, 2)

    fields = [planes_of(vectors[:, :, :, y]) for y in range(y_rows)] + [
        planes_of(incoming[:, :, :, 0])
    ]
    y_links = gauge_links[0].astype(F32)

    chosen = perambulators[source_times]
    sources, sinks, spins, _, own_rows, _ = chosen.shape
    chosen_re, chosen_im = chosen[:, :, :, 0], chosen[:, :, :, 1]
    rows = sources * sinks * spins * own_rows
    contract_left = jnp.stack(
        [
            jnp.concatenate([chosen_re, -chosen_im], axis=-1),
            jnp.concatenate([chosen_im, chosen_re], axis=-1),
        ],
        axis=-2,
    ).reshape(2 * rows, 2 * vec_count)

    norm_factor = 1.0 / math.sqrt(6 * y_total * site_count)
    order = list(range(bits))
    out = None
    shape = (rows, path_total, mom_count, 2, vec_count)
    blocks = []
    for path in range(path_total):
        total = None
        for y in range(y_rows):
            z_next = z_links[:, :, :, y + 1] if y + 1 < y_rows else z_incoming[:, :, :, 0]
            table = path_tables(
                y_links[:, :, :, y],
                z_links[:, :, :, y],
                z_next,
                momenta,
                path_codes[path],
                lax.axis_index("gy") * y_rows + y,
                y_total,
            )
            part = partial_elemental(
                path_codes[path], fields[y], fields[y + 1], table, mom_count
            )
            total = part if total is None else total + part
        owned = scatter_rows(total, "gy", order)
        blocks.append(gather_rows((owned * norm_factor).astype(BF16), "gy", order))
    for path in range(path_total):
        out = contract(path, contract_left, blocks[path], shape, out)
    return out.reshape(
        sources, sinks, spins, own_rows, path_total, mom_count, 2, vec_count
    )


def solution(mesh):
    placed = (
        P("grp", None, None, "gy", None),
        P("grp", None, None, None, "gy", None),
        P("grp", None, None, None, "gy", None),
        P(),
        P(),
        P("grp"),
    )
    return jax.shard_map(
        shards,
        mesh=mesh,
        in_specs=placed,
        out_specs=P("grp", None, None, "gy", None, None, None, None),
        check_vma=False,
    )
```

```python
import functools
import math

import jax
import jax.numpy as jnp
from jax import lax
from jax.experimental import pallas as pl
from jax.experimental.pallas import tpu as pltpu
from jax.sharding import PartitionSpec as P

LX = 32
LZ = 16
LANES = 128
ROWS = 16
TWO_PI = 6.283185307179586

F32 = jnp.float32
BF16 = jnp.bfloat16
NT = (((1,), (1,)), ((), ()))


def matrix_rows(link, base, dagger):
    rows = {}
    for row in range(3):
        for col in range(3):
            at = col * 3 + row if dagger else row * 3 + col
            real_part = link[base + at : base + at + 1, :].astype(F32)
            imag_part = link[base + 9 + at : base + 10 + at, :].astype(F32)
            rows[row, col] = (real_part, -imag_part if dagger else imag_part)
    return rows


def roll_sites(field, shift):
    sites = field.shape[-1]
    return jnp.concatenate([field[:, sites - shift :], field[:, : sites - shift]], axis=1)


def write_matrix(links, z_next, table, path, ahead_y, ahead_z):
    step_y = matrix_rows(links, 0, not ahead_y)
    step_z = matrix_rows(links, 18, not ahead_z) if ahead_y else matrix_rows(z_next, 0, not ahead_z)
    if ahead_z:
        step_z = {k: (roll_sites(v[0], LX), roll_sites(v[1], LX)) for k, v in step_z.items()}
    for row in range(3):
        for col in range(3):
            real_part = imag_part = None
            for mid in range(3):
                l_re, l_im = step_z[row, mid]
                r_re, r_im = step_y[mid, col]
                term_re = l_re * r_re - l_im * r_im
                term_im = l_re * r_im + l_im * r_re
                real_part = term_re if real_part is None else real_part + term_re
                imag_part = term_im if imag_part is None else imag_part + term_im
            at = row * 3 + col
            table[path, at : at + 1, :] = real_part
            table[path, 9 + at : 10 + at, :] = imag_part


def write_phases(momenta, codes, y_coord, table, path, y_total):
    mom_count, sites = momenta.shape[0], table.shape[2]
    ahead_y, ahead_z = codes[path, 0] == 1, codes[path, 1] == 1
    positions = lax.broadcasted_iota(jnp.int32, (1, sites), 1)
    positions = lax.rem(positions + jnp.where(ahead_z, sites - LX, LX), sites)
    y_here = lax.rem(jnp.where(ahead_y, y_coord, y_coord + 1), y_total)
    period = LX * y_total * LZ
    x_part = lax.rem(positions, LX) * (y_total * LZ)
    z_part = lax.div(positions, LX) * (LX * y_total)
    for mom in range(mom_count):
        raw = (
            momenta[mom, 0] * x_part
            + momenta[mom, 1] * y_here * (LX * LZ)
            + momenta[mom, 2] * z_part
        )
        residue = lax.rem(raw, period)
        residue = jnp.where(residue < 0, residue + period, residue)
        angle = residue.astype(F32) * (TWO_PI / period)
        table[path, 18 + mom : 19 + mom, :] = jnp.cos(angle)
        table[path, 18 + mom_count + mom : 19 + mom_count + mom, :] = jnp.sin(angle)


def build_left(source, ahead_z, left):
    planes, count, sites = source.shape
    half = planes // 2
    for plane in range(planes):
        field = roll_sites(source[plane], LX if ahead_z else sites - LX)
        left[:count, plane * sites : (plane + 1) * sites] = field
        other = ((plane + half) % planes) * sites
        left[count : 2 * count, other : other + sites] = field if plane < half else -field


def build_right(source, table, path, right, mom_count):
    planes, count, sites = source.shape
    for lane in range(0, sites, LANES):
        cols = slice(lane, lane + LANES)
        rows = [
            jnp.broadcast_to(table[path, k : k + 1, cols], (ROWS, LANES))
            for k in range(18 + 2 * mom_count)
        ]

        def step(group, carry):
            start = pl.multiple_of(group * ROWS, ROWS)
            field = [source[plane, pl.ds(start, ROWS), cols].astype(F32) for plane in range(6)]
            for out in range(3):
                real_part = imag_part = None
                for col in range(3):
                    m_re, m_im = rows[out * 3 + col], rows[9 + out * 3 + col]
                    v_re, v_im = field[col], field[3 + col]
                    term_re = m_re * v_re - m_im * v_im
                    term_im = m_re * v_im + m_im * v_re
                    real_part = term_re if real_part is None else real_part + term_re
                    imag_part = term_im if imag_part is None else imag_part + term_im
                for mom in range(mom_count):
                    cosine, sine = rows[18 + mom], rows[18 + mom_count + mom]
                    dest = pl.ds(pl.multiple_of(mom * count + start, ROWS), ROWS)
                    at = out * sites + lane
                    right[dest, at : at + LANES] = (
                        cosine * real_part + sine * imag_part
                    ).astype(BF16)
                    at += 3 * sites
                    right[dest, at : at + LANES] = (
                        cosine * imag_part - sine * real_part
                    ).astype(BF16)
            return carry

        lax.fori_loop(0, count // ROWS, step, 0)


def by_code(value, body):
    for ahead in (False, True):
        pl.when((value == 1) == ahead)(functools.partial(body, ahead))


def local_kernel(y_total, codes, momenta, y_coord, here, links, z_next, table, *fixed):
    mom_count = momenta.shape[0]
    for path, factor in enumerate(fixed):
        write_phases(momenta, codes, y_coord[0], table, path, y_total)

        def along_y(ahead_y):
            by_code(
                codes[path, 1],
                lambda ahead_z: write_matrix(links, z_next, table, path, ahead_y, ahead_z),
            )
            if ahead_y:
                by_code(codes[path, 1], lambda ahead_z: build_left(here, ahead_z, factor))
            else:
                build_right(here, table, path, factor, mom_count)

        by_code(codes[path, 0], along_y)


def local_factors(codes, momenta, y_coord, here, links, z_next, y_total):
    planes, count, sites = here.shape
    mom_count, paths = momenta.shape[0], codes.shape[0]
    height = max(2, mom_count) * count
    return pl.pallas_call(
        functools.partial(local_kernel, y_total),
        out_shape=[jax.ShapeDtypeStruct((paths, 18 + 2 * mom_count, sites), F32)]
        + [jax.ShapeDtypeStruct((height, planes * sites), BF16)] * paths,
        in_specs=[pl.BlockSpec(memory_space=pltpu.SMEM)] * 3
        + [pl.BlockSpec(memory_space=pltpu.VMEM)] * 3,
        out_specs=[pl.BlockSpec(memory_space=pltpu.VMEM)] * (paths + 1),
        compiler_params=pltpu.CompilerParams(vmem_limit_bytes=24 << 20),
        cost_estimate=pl.CostEstimate(flops=10**9, bytes_accessed=14 << 20, transcendentals=0),
        name="local",
    )(codes, momenta, y_coord, here, links, z_next)


def chunk_kernel(mom_count, *refs):
    codes, half, after, table = refs[:4]
    paths = codes.shape[0]
    fixed = refs[4 : 4 + paths]
    kept, sent, moving, product = refs[4 + paths :]
    width = after.shape[1]
    rows = kept.shape[0]
    count = 2 * rows
    mine = pl.multiple_of(half[0] * rows, rows)
    other = pl.multiple_of((1 - half[0]) * rows, rows)
    span = 2 * mom_count * width
    for path in range(paths):
        factor = fixed[path]

        def along_y(ahead_y):
            if ahead_y:
                build_right(after, table, path, moving, mom_count)
                product[...] = lax.dot_general(
                    factor[: 2 * count], moving[...], NT, preferred_element_type=F32
                ).reshape(product.shape)
                for mom in range(mom_count):
                    for part in range(2):
                        to = path * span + (2 * mom + part) * width
                        at = part * count
                        cols = slice(mom * width, (mom + 1) * width)
                        kept[:, to : to + width] = product[pl.ds(at + mine, rows), cols]
                        sent[:, to : to + width] = product[pl.ds(at + other, rows), cols].astype(
                            BF16
                        )
            else:
                by_code(codes[path, 1], lambda ahead_z: build_left(after, ahead_z, moving))
                for mom in range(mom_count):
                    values = lax.dot_general(
                        factor[mom * count : (mom + 1) * count],
                        moving[: 2 * width],
                        NT,
                        preferred_element_type=F32,
                    )
                    product[:count, : 2 * width] = values
                    to = path * span + 2 * mom * width
                    kept[:, to : to + 2 * width] = product[pl.ds(mine, rows), : 2 * width]
                    sent[:, to : to + 2 * width] = product[pl.ds(other, rows), : 2 * width].astype(
                        BF16
                    )

        by_code(codes[path, 0], along_y)


def chunk_partials(codes, half, after, table, fixed, mom_count, count, name):
    planes, width, sites = after.shape
    paths = codes.shape[0]
    span = paths * 2 * mom_count * width
    return pl.pallas_call(
        functools.partial(chunk_kernel, mom_count),
        out_shape=[
            jax.ShapeDtypeStruct((count // 2, span), F32),
            jax.ShapeDtypeStruct((count // 2, span), BF16),
        ],
        in_specs=[pl.BlockSpec(memory_space=pltpu.SMEM)] * 2
        + [pl.BlockSpec(memory_space=pltpu.VMEM)] * (2 + paths),
        out_specs=[pl.BlockSpec(memory_space=pltpu.VMEM)] * 2,
        scratch_shapes=[
            pltpu.VMEM((max(2, mom_count) * width, planes * sites), BF16),
            pltpu.VMEM((2 * count, max(2, mom_count) * width), F32),
        ],
        compiler_params=pltpu.CompilerParams(vmem_limit_bytes=26 << 20),
        cost_estimate=pl.CostEstimate(
            flops=2 * count * span * planes * sites, bytes_accessed=8 << 20, transcendentals=0
        ),
        name=name,
    )(codes, half, after, table, *fixed)


def swap_pairs(count, bit):
    return [(i, i ^ (1 << bit)) for i in range(count)]


def sum_rows(kept, sent, axis, order):
    me, count = lax.axis_index(axis), lax.axis_size(axis)
    for level, bit in enumerate(order):
        cells = kept + lax.ppermute(sent, axis, swap_pairs(count, bit)).astype(F32)
        if level + 1 == len(order):
            return cells
        following = order[level + 1]
        if level + 2 == len(order):
            kept, sent = cells, cells.astype(BF16)
        else:
            half = cells.shape[0] // 2
            mine = (me >> following) & 1
            kept = lax.dynamic_slice_in_dim(cells, mine * half, half, 0)
            sent = lax.dynamic_slice_in_dim(cells, (1 - mine) * half, half, 0).astype(BF16)


def gather_rows(cells, axis, order):
    me, count = lax.axis_index(axis), lax.axis_size(axis)
    for bit in reversed(order[:-1]):
        other = lax.ppermute(cells, axis, swap_pairs(count, bit))
        upper = ((me >> bit) & 1) == 1
        cells = jnp.concatenate(
            [jnp.where(upper, other, cells), jnp.where(upper, cells, other)], axis=0
        )
    return cells


def contract_kernel(codes, left, *refs):
    blocks, (out, tiles, sems) = refs[:-3], refs[-3:]
    paths, mom_count, count = out.shape[1], out.shape[2], out.shape[4]
    row_count = out.shape[0]
    chunks = len(blocks)
    width = count // chunks

    def slot(path, mom, lane):
        return (path * mom_count + mom) * (count // LANES) + lane // LANES

    def copy(path, mom, lane):
        at = slot(path, mom, lane)
        return pltpu.make_async_copy(
            tiles.at[at], out.at[:, path, mom, :, lane : lane + LANES], sems.at[at]
        )

    for path in range(paths):

        def along_y(ahead_y):
            for mom in range(mom_count):
                at = (path * mom_count + mom) * 2 * width
                product = None
                if ahead_y:
                    pieces = []
                    for part in range(chunks):
                        for side in range(2):
                            cols = slice(at + side * width, at + (side + 1) * width)
                            span = slice(part * width, (part + 1) * width)
                            pieces.append(
                                jnp.concatenate([block[span, cols] for block in blocks], axis=1)
                            )
                    product = jnp.dot(
                        left[...], jnp.concatenate(pieces, axis=0), preferred_element_type=F32
                    )
                else:
                    for part, block in enumerate(blocks):
                        term = lax.dot_general(
                            left[:, part * 2 * width : (part + 1) * 2 * width],
                            block[:, at : at + 2 * width],
                            NT,
                            preferred_element_type=F32,
                        )
                        product = term if product is None else product + term
                product = product.astype(BF16)
                for lane in range(0, count, LANES):
                    tiles[slot(path, mom, lane)] = product[:, lane : lane + LANES].reshape(
                        row_count, 2, LANES
                    )
                    copy(path, mom, lane).start()

        by_code(codes[path, 0], along_y)
    for path in range(paths):
        for mom in range(mom_count):
            for lane in range(0, count, LANES):
                copy(path, mom, lane).wait()


def contract(codes, left, blocks, shape):
    slots = shape[1] * shape[2] * (shape[4] // LANES)
    return pl.pallas_call(
        contract_kernel,
        out_shape=jax.ShapeDtypeStruct(shape, BF16),
        in_specs=[pl.BlockSpec(memory_space=pltpu.SMEM)]
        + [pl.BlockSpec(memory_space=pltpu.VMEM)] * (1 + len(blocks)),
        out_specs=pl.BlockSpec(memory_space=pl.ANY),
        scratch_shapes=[
            pltpu.VMEM((slots, shape[0], 2, LANES), BF16),
            pltpu.SemaphoreType.DMA((slots,)),
        ],
        compiler_params=pltpu.CompilerParams(vmem_limit_bytes=24 << 20),
        cost_estimate=pl.CostEstimate(
            flops=8 * math.prod(shape), bytes_accessed=8 << 20, transcendentals=0
        ),
        name="contract",
    )(codes, left, *blocks)


def shards(vectors, gauge_links, perambulators, momenta, path_codes, source_times):
    vec_count, _, _, y_rows, site_count = vectors.shape
    y_devices = lax.axis_size("gy")
    y_total = y_rows * y_devices
    mom_count, path_total = momenta.shape[0], path_codes.shape[0]
    bits = y_devices.bit_length() - 1
    down = [((i + 1) % y_devices, i) for i in range(y_devices)]
    me = lax.axis_index("gy")
    chunks = vec_count // LANES

    def planes_of(field):
        return field.reshape(field.shape[0], 6, site_count).transpose(1, 0, 2)

    z_incoming = lax.ppermute(gauge_links[1][:, :, :, :1], "gy", down)
    incoming = [
        lax.ppermute(vectors[c * LANES : (c + 1) * LANES, :, :, :1], "gy", down)
        for c in range(chunks)
    ]
    half = (me & 1).astype(jnp.int32).reshape(1)
    kept, sent = [None] * chunks, [None] * chunks
    for y in range(y_rows):
        inside = y + 1 < y_rows
        z_next = gauge_links[1][:, :, :, y + 1] if inside else z_incoming[:, :, :, 0]
        table, *fixed = local_factors(
            path_codes,
            momenta,
            (me * y_rows + y).astype(jnp.int32).reshape(1),
            planes_of(vectors[:, :, :, y]),
            gauge_links[:, :, :, :, y].reshape(36, site_count),
            z_next.reshape(18, site_count),
            y_total,
        )
        for c in range(chunks):
            after = (
                vectors[c * LANES : (c + 1) * LANES, :, :, y + 1]
                if inside
                else incoming[c][:, :, :, 0]
            )
            with jax.named_scope(f"chunk{c}"):
                new_kept, new_sent = chunk_partials(
                    path_codes, half, planes_of(after), table, fixed, mom_count, vec_count,
                    f"chunk{c}",
                )
            if kept[c] is None:
                kept[c], sent[c] = new_kept, new_sent
            else:
                kept[c] = kept[c] + new_kept
                sent[c] = (sent[c].astype(F32) + new_sent.astype(F32)).astype(BF16)

    chosen = perambulators[source_times]
    sources, sinks, spins, _, own_rows, _ = chosen.shape
    rows = sources * sinks * spins * own_rows
    chosen_re, chosen_im = [
        chosen[:, :, :, part].reshape(rows, chunks, 1, LANES) for part in range(2)
    ]
    contract_left = jnp.stack(
        [
            jnp.concatenate([chosen_re, -chosen_im], axis=2),
            jnp.concatenate([chosen_im, chosen_re], axis=2),
        ],
        axis=1,
    ).reshape(2 * rows, 2 * vec_count)

    norm_factor = 1.0 / math.sqrt(6 * y_total * site_count)
    blocks = []
    for c in range(chunks):
        order = list(range(bits)) if c % 2 == 0 else [0] + list(range(2, bits)) + [1]
        with jax.named_scope(f"sum{c}"):
            owned = sum_rows(kept[c], sent[c], "gy", order)
        with jax.named_scope(f"gather{c}"):
            blocks.append(gather_rows((owned * norm_factor).astype(BF16), "gy", order))
    out = contract(
        path_codes, contract_left, blocks, (rows, path_total, mom_count, 2, vec_count)
    )
    return out.reshape(
        sources, sinks, spins, own_rows, path_total, mom_count, 2, vec_count
    )


def solution(mesh):
    placed = (
        P("grp", None, None, "gy", None),
        P("grp", None, None, None, "gy", None),
        P("grp", None, None, None, "gy", None),
        P(),
        P(),
        P("grp"),
    )
    return jax.shard_map(
        shards,
        mesh=mesh,
        in_specs=placed,
        out_specs=P("grp", None, None, "gy", None, None, None, None),
        check_vma=False,
    )
```

```python
import functools
import math

import jax
import jax.numpy as jnp
from jax import lax
from jax.experimental import pallas as pl
from jax.experimental.pallas import tpu as pltpu
from jax.sharding import PartitionSpec as P


LX = 32
LZ = 16
LANES = 128
ROWS = 16
TWO_PI = 6.283185307179586

F32 = jnp.float32
BF16 = jnp.bfloat16
NT = (((1,), (1,)), ((), ()))


def matrix_rows(link, base, dagger):
    rows = {}
    for row in range(3):
        for col in range(3):
            at = col * 3 + row if dagger else row * 3 + col
            real_part = link[base + at : base + at + 1, :].astype(F32)
            imag_part = link[base + 9 + at : base + 10 + at, :].astype(F32)
            rows[row, col] = (real_part, -imag_part if dagger else imag_part)
    return rows


def roll_sites(field, shift):
    sites = field.shape[-1]
    return jnp.concatenate([field[:, sites - shift :], field[:, : sites - shift]], axis=1)


def write_matrix(links, z_next, table, path, ahead_y, ahead_z):
    step_y = matrix_rows(links, 0, not ahead_y)
    step_z = matrix_rows(links, 18, not ahead_z) if ahead_y else matrix_rows(z_next, 0, not ahead_z)
    if ahead_z:
        step_z = {k: (roll_sites(v[0], LX), roll_sites(v[1], LX)) for k, v in step_z.items()}
    for row in range(3):
        for col in range(3):
            real_part = imag_part = None
            for mid in range(3):
                l_re, l_im = step_z[row, mid]
                r_re, r_im = step_y[mid, col]
                term_re = l_re * r_re - l_im * r_im
                term_im = l_re * r_im + l_im * r_re
                real_part = term_re if real_part is None else real_part + term_re
                imag_part = term_im if imag_part is None else imag_part + term_im
            at = row * 3 + col
            table[path, at : at + 1, :] = real_part
            table[path, 9 + at : 10 + at, :] = imag_part


def write_phases(momenta, codes, y_coord, table, path, y_total):
    mom_count, sites = momenta.shape[0], table.shape[2]
    ahead_y, ahead_z = codes[path, 0] == 1, codes[path, 1] == 1
    positions = lax.broadcasted_iota(jnp.int32, (1, sites), 1)
    positions = lax.rem(positions + jnp.where(ahead_z, sites - LX, LX), sites)
    y_here = lax.rem(jnp.where(ahead_y, y_coord, y_coord + 1), y_total)
    period = LX * y_total * LZ
    x_part = lax.rem(positions, LX) * (y_total * LZ)
    z_part = lax.div(positions, LX) * (LX * y_total)
    for mom in range(mom_count):
        raw = (
            momenta[mom, 0] * x_part
            + momenta[mom, 1] * y_here * (LX * LZ)
            + momenta[mom, 2] * z_part
        )
        residue = lax.rem(raw, period)
        residue = jnp.where(residue < 0, residue + period, residue)
        angle = residue.astype(F32) * (TWO_PI / period)
        table[path, 18 + mom : 19 + mom, :] = jnp.cos(angle)
        table[path, 18 + mom_count + mom : 19 + mom_count + mom, :] = jnp.sin(angle)


def build_left(sources, ahead_z, left):
    planes, width, sites = sources[0].shape
    half = planes // 2
    count = width * len(sources)
    for index, source in enumerate(sources):
        base = index * width
        for plane in range(planes):
            field = roll_sites(source[plane], LX if ahead_z else sites - LX)
            left[base : base + width, plane * sites : (plane + 1) * sites] = field
            other = ((plane + half) % planes) * sites
            left[count + base : count + base + width, other : other + sites] = (
                field if plane < half else -field
            )


def build_right(sources, table, path, right, mom_count):
    _, width, sites = sources[0].shape
    count = width * len(sources)
    for lane in range(0, sites, LANES):
        cols = slice(lane, lane + LANES)
        rows = [
            jnp.broadcast_to(table[path, k : k + 1, cols], (ROWS, LANES))
            for k in range(18 + 2 * mom_count)
        ]
        for index, source in enumerate(sources):

            def step(group, carry):
                start = pl.multiple_of(group * ROWS, ROWS)
                field = [source[plane, pl.ds(start, ROWS), cols].astype(F32) for plane in range(6)]
                for out in range(3):
                    real_part = imag_part = None
                    for col in range(3):
                        m_re, m_im = rows[out * 3 + col], rows[9 + out * 3 + col]
                        v_re, v_im = field[col], field[3 + col]
                        term_re = m_re * v_re - m_im * v_im
                        term_im = m_re * v_im + m_im * v_re
                        real_part = term_re if real_part is None else real_part + term_re
                        imag_part = term_im if imag_part is None else imag_part + term_im
                    for mom in range(mom_count):
                        cosine, sine = rows[18 + mom], rows[18 + mom_count + mom]
                        dest = mom * count + index * width + start
                        dest = pl.ds(pl.multiple_of(dest, ROWS), ROWS)
                        at = out * sites + lane
                        right[dest, at : at + LANES] = (
                            cosine * real_part + sine * imag_part
                        ).astype(BF16)
                        at += 3 * sites
                        right[dest, at : at + LANES] = (
                            cosine * imag_part - sine * real_part
                        ).astype(BF16)
                return carry

            lax.fori_loop(0, width // ROWS, step, 0)


def by_code(value, body):
    for ahead in (False, True):
        pl.when((value == 1) == ahead)(functools.partial(body, ahead))


def parting(size, apart):
    row = lax.broadcasted_iota(jnp.int32, (size, size), 0)
    col = lax.broadcasted_iota(jnp.int32, (size, size), 1)
    if not apart:
        row, col = col, row
    half = size // 2
    source = jnp.where(row < half, 2 * row, 2 * (row - half) + 1)
    return jnp.where(col == source, 1.0, 0.0).astype(BF16)


def planes_kernel(raw, out):
    width, colors, _, sites = raw.shape
    apart = parting(2 * width, True)
    for color in range(colors):
        for lane in range(0, sites, LANES):
            cols = slice(lane, lane + LANES)
            rows = raw[:, color, :, cols].reshape(2 * width, LANES)
            parted = jnp.dot(apart, rows, preferred_element_type=F32).astype(BF16)
            out[color, :, cols] = parted[:width]
            out[colors + color, :, cols] = parted[width:]


def planes_of(raw, chunk):
    _, colors, parts, sites = raw.shape
    return pl.pallas_call(
        planes_kernel,
        grid=(1,),
        out_shape=jax.ShapeDtypeStruct((parts * colors, LANES, sites), BF16),
        in_specs=[pl.BlockSpec((LANES, colors, parts, sites), lambda i: (chunk, 0, 0, 0))],
        out_specs=pl.BlockSpec((parts * colors, LANES, sites), lambda i: (0, 0, 0)),
        compiler_params=pltpu.CompilerParams(vmem_limit_bytes=8 << 20),
        cost_estimate=pl.CostEstimate(flops=10**8, bytes_accessed=2 << 20, transcendentals=0),
        name="planes",
    )(raw)


def local_kernel(y_total, chunks, codes, momenta, y_coord, times, *refs):
    here, (links, z_next, stored, table, fixed, left, chosen, sems) = refs[:chunks], refs[chunks:]
    mom_count, paths = momenta.shape[0], codes.shape[0]
    sources, sinks, spins, _, own, count = chosen.shape
    copies = [
        pltpu.make_async_copy(stored.at[times[i]], chosen.at[i], sems.at[i])
        for i in range(sources)
    ]
    for copy in copies:
        copy.start()

    def one_path(path, carry):
        factor = fixed.at[path]
        write_phases(momenta, codes, y_coord[0], table, path, y_total)

        def along_y(ahead_y):
            by_code(
                codes[path, 1],
                lambda ahead_z: write_matrix(links, z_next, table, path, ahead_y, ahead_z),
            )
            if ahead_y:
                by_code(codes[path, 1], lambda ahead_z: build_left(here, ahead_z, factor))
            else:
                build_right(here, table, path, factor, mom_count)

        by_code(codes[path, 0], along_y)
        return carry

    lax.fori_loop(0, paths, one_path, 0)
    for copy in copies:
        copy.wait()
    together = parting(2 * sinks * spins * own, False)
    for source in range(sources):
        real_rows, imag_rows = [
            jnp.concatenate(
                [chosen[source, sink, spin, part] for sink in range(sinks) for spin in range(spins)],
                axis=0,
            )
            for part in range(2)
        ]
        upper, lower = [], []
        for at in range(0, count, LANES):
            re, im = real_rows[:, at : at + LANES], imag_rows[:, at : at + LANES]
            upper += [re, -im]
            lower += [im, re]
        rows = jnp.concatenate(
            [jnp.concatenate(upper, axis=1), jnp.concatenate(lower, axis=1)], axis=0
        )
        height = rows.shape[0]
        left[source * height : (source + 1) * height] = jnp.dot(
            together, rows, preferred_element_type=F32
        ).astype(BF16)


def local_factors(codes, momenta, y_coord, times, here, links, z_next, stored, y_total):
    planes, width, sites = here[0].shape
    count = width * len(here)
    mom_count, paths, sources = momenta.shape[0], codes.shape[0], times.shape[0]
    height = max(2, mom_count) * count
    _, sinks, spins, _, own, _ = stored.shape
    return pl.pallas_call(
        functools.partial(local_kernel, y_total, len(here)),
        out_shape=[
            jax.ShapeDtypeStruct((paths, 18 + 2 * mom_count, sites), F32),
            jax.ShapeDtypeStruct((paths, height, planes * sites), BF16),
            jax.ShapeDtypeStruct((2 * sources * sinks * spins * own, 2 * count), BF16),
        ],
        in_specs=[pl.BlockSpec(memory_space=pltpu.SMEM)] * 4
        + [pl.BlockSpec(memory_space=pltpu.VMEM)] * (len(here) + 2)
        + [pl.BlockSpec(memory_space=pl.ANY)],
        out_specs=[pl.BlockSpec(memory_space=pltpu.VMEM)] * 3,
        scratch_shapes=[
            pltpu.VMEM((sources,) + stored.shape[1:], BF16),
            pltpu.SemaphoreType.DMA((sources,)),
        ],
        compiler_params=pltpu.CompilerParams(vmem_limit_bytes=20 << 20),
        cost_estimate=pl.CostEstimate(flops=10**9, bytes_accessed=14 << 20, transcendentals=0),
        name="local",
    )(codes, momenta, y_coord, times, *here, links, z_next, stored)


def chunk_kernel(mom_count, codes, half, after, table, fixed, kept, sent, moving, product):
    paths = codes.shape[0]
    width = after.shape[1]
    rows = kept.shape[0]
    count = 2 * rows
    mine = pl.multiple_of(half[0] * rows, rows)
    other = pl.multiple_of((1 - half[0]) * rows, rows)
    span = 2 * mom_count * width

    def one_path(path, carry):
        factor = fixed.at[path]
        base = path * span

        def along_y(ahead_y):
            if ahead_y:
                build_right([after], table, path, moving, mom_count)
                product[...] = lax.dot_general(
                    factor[: 2 * count], moving[...], NT, preferred_element_type=F32
                )
                for mom in range(mom_count):
                    for part in range(2):
                        to = pl.multiple_of(base + (2 * mom + part) * width, LANES)
                        at = part * count
                        cols = slice(mom * width, (mom + 1) * width)
                        kept[:, pl.ds(to, width)] = product[pl.ds(at + mine, rows), cols]
                        sent[:, pl.ds(to, width)] = product[pl.ds(at + other, rows), cols].astype(
                            BF16
                        )
            else:
                by_code(codes[path, 1], lambda ahead_z: build_left([after], ahead_z, moving))
                for mom in range(mom_count):
                    product[:count, : 2 * width] = lax.dot_general(
                        factor[mom * count : (mom + 1) * count],
                        moving[: 2 * width],
                        NT,
                        preferred_element_type=F32,
                    )
                    to = pl.multiple_of(base + 2 * mom * width, LANES)
                    kept[:, pl.ds(to, 2 * width)] = product[pl.ds(mine, rows), : 2 * width]
                    sent[:, pl.ds(to, 2 * width)] = product[
                        pl.ds(other, rows), : 2 * width
                    ].astype(BF16)

        by_code(codes[path, 0], along_y)
        return carry

    lax.fori_loop(0, paths, one_path, 0)


def chunk_partials(codes, half, after, table, fixed, mom_count, count):
    planes, width, sites = after.shape
    paths = codes.shape[0]
    span = paths * 2 * mom_count * width
    return pl.pallas_call(
        functools.partial(chunk_kernel, mom_count),
        out_shape=[
            jax.ShapeDtypeStruct((count // 2, span), F32),
            jax.ShapeDtypeStruct((count // 2, span), BF16),
        ],
        in_specs=[pl.BlockSpec(memory_space=pltpu.SMEM)] * 2
        + [pl.BlockSpec(memory_space=pltpu.VMEM)] * 3,
        out_specs=[pl.BlockSpec(memory_space=pltpu.VMEM)] * 2,
        scratch_shapes=[
            pltpu.VMEM((max(2, mom_count) * width, planes * sites), BF16),
            pltpu.VMEM((2 * count, max(2, mom_count) * width), F32),
        ],
        compiler_params=pltpu.CompilerParams(vmem_limit_bytes=20 << 20),
        cost_estimate=pl.CostEstimate(
            flops=2 * count * span * planes * sites, bytes_accessed=8 << 20, transcendentals=0
        ),
        name="chunk",
    )(codes, half, after, table, fixed)


def swap_pairs(count, bit):
    return [(i, i ^ (1 << bit)) for i in range(count)]


def sum_rows(kept, sent, axis, order):
    me, count = lax.axis_index(axis), lax.axis_size(axis)
    for level, bit in enumerate(order):
        cells = kept + lax.ppermute(sent, axis, swap_pairs(count, bit)).astype(F32)
        if level + 1 == len(order):
            return cells
        following = order[level + 1]
        if level + 2 == len(order):
            kept, sent = cells, cells.astype(BF16)
        else:
            half = cells.shape[0] // 2
            mine = (me >> following) & 1
            kept = lax.dynamic_slice_in_dim(cells, mine * half, half, 0)
            sent = lax.dynamic_slice_in_dim(cells, (1 - mine) * half, half, 0).astype(BF16)


def gather_rows(cells, axis, order):
    me, count = lax.axis_index(axis), lax.axis_size(axis)
    for bit in reversed(order[:-1]):
        other = lax.ppermute(cells, axis, swap_pairs(count, bit))
        mine = lax.broadcasted_iota(jnp.int32, (2, 1, 1), 0) == ((me >> bit) & 1)
        cells = jnp.where(mine, cells[None], other[None]).reshape(2 * cells.shape[0], -1)
    return cells


def contract_kernel(codes, left, *refs):
    blocks, (out, tiles, sems) = refs[:-3], refs[-3:]
    row_count, paths, mom_count, _, count = out.shape
    width = count // len(blocks)

    def copy(path):
        return pltpu.make_async_copy(tiles.at[:, path], out.at[:, path], sems.at[path])

    def one_path(path, carry):
        def along_y(ahead_y):
            for mom in range(mom_count):
                at = path * mom_count * 2 * width + mom * 2 * width
                product = None
                if ahead_y:
                    pieces = []
                    for part in range(len(blocks)):
                        for side in range(2):
                            cols = pl.ds(pl.multiple_of(at + side * width, LANES), width)
                            span = slice(part * width, (part + 1) * width)
                            pieces.append(
                                jnp.concatenate([block[span, cols] for block in blocks], axis=1)
                            )
                    product = jnp.dot(
                        left[...], jnp.concatenate(pieces, axis=0), preferred_element_type=F32
                    )
                else:
                    for part, block in enumerate(blocks):
                        term = lax.dot_general(
                            left[:, part * 2 * width : (part + 1) * 2 * width],
                            block[:, pl.ds(pl.multiple_of(at, LANES), 2 * width)],
                            NT,
                            preferred_element_type=F32,
                        )
                        product = term if product is None else product + term
                product = product.astype(BF16)
                for lane in range(0, count, LANES):
                    tiles[:, path, mom, :, lane : lane + LANES] = product[
                        :, lane : lane + LANES
                    ].reshape(row_count, 2, LANES)

        by_code(codes[path, 0], along_y)
        copy(path).start()
        return carry

    lax.fori_loop(0, paths, one_path, 0)
    for path in range(paths):
        copy(path).wait()


def contract(codes, left, blocks, shape):
    return pl.pallas_call(
        contract_kernel,
        out_shape=jax.ShapeDtypeStruct(shape, BF16),
        in_specs=[pl.BlockSpec(memory_space=pltpu.SMEM)]
        + [pl.BlockSpec(memory_space=pltpu.VMEM)] * (1 + len(blocks)),
        out_specs=pl.BlockSpec(memory_space=pl.ANY),
        scratch_shapes=[pltpu.VMEM(shape, BF16), pltpu.SemaphoreType.DMA((shape[1],))],
        compiler_params=pltpu.CompilerParams(vmem_limit_bytes=20 << 20),
        cost_estimate=pl.CostEstimate(
            flops=8 * math.prod(shape), bytes_accessed=8 << 20, transcendentals=0
        ),
        name="contract",
    )(codes, left, *blocks)


def shards(vectors, gauge_links, perambulators, momenta, path_codes, source_times):
    vec_count, _, _, y_rows, site_count = vectors.shape
    y_devices = lax.axis_size("gy")
    y_total = y_rows * y_devices
    mom_count, path_total = momenta.shape[0], path_codes.shape[0]
    bits = y_devices.bit_length() - 1
    down = [((i + 1) % y_devices, i) for i in range(y_devices)]
    me = lax.axis_index("gy")
    chunks = vec_count // LANES

    raw = vectors.transpose(0, 2, 3, 1, 4)
    fields = [[planes_of(raw[:, :, y], c) for c in range(chunks)] for y in range(y_rows)]
    z_incoming = lax.ppermute(gauge_links[1][:, :, :, :1], "gy", down)
    incoming = []
    for c in range(chunks):
        incoming.append(lax.ppermute(fields[0][c], "gy", down))
    fields.append(incoming)
    half = (me & 1).astype(jnp.int32).reshape(1)
    kept, sent = [None] * chunks, [None] * chunks
    for y in range(y_rows):
        inside = y + 1 < y_rows
        z_next = gauge_links[1][:, :, :, y + 1] if inside else z_incoming[:, :, :, 0]
        table, fixed, contract_left = local_factors(
            path_codes,
            momenta,
            (me * y_rows + y).astype(jnp.int32).reshape(1),
            source_times,
            fields[y],
            gauge_links[:, :, :, :, y].reshape(36, site_count),
            z_next.reshape(18, site_count),
            perambulators,
            y_total,
        )
        for c in range(chunks):
            new_kept, new_sent = chunk_partials(
                path_codes, half, fields[y + 1][c], table, fixed, mom_count, vec_count
            )
            if kept[c] is None:
                kept[c], sent[c] = new_kept, new_sent
            else:
                kept[c] = kept[c] + new_kept
                sent[c] = (sent[c].astype(F32) + new_sent.astype(F32)).astype(BF16)

    norm_factor = 1.0 / math.sqrt(6 * y_total * site_count)
    blocks = []
    for c in range(chunks):
        order = list(range(bits)) if c % 2 == 0 else [0] + list(range(2, bits)) + [1]
        owned = sum_rows(kept[c], sent[c], "gy", order)
        blocks.append(gather_rows((owned * norm_factor).astype(BF16), "gy", order))
    sources, (_, sinks, spins, _, own_rows, _) = source_times.shape[0], perambulators.shape
    rows = sources * sinks * spins * own_rows
    out = contract(
        path_codes, contract_left, blocks, (rows, path_total, mom_count, 2, vec_count)
    )
    return out.reshape(
        sources, sinks, spins, own_rows, path_total, mom_count, 2, vec_count
    )


def solution(mesh):
    placed = (
        P("grp", None, None, "gy", None),
        P("grp", None, None, None, "gy", None),
        P("grp", None, None, None, "gy", None),
        P(),
        P(),
        P("grp"),
    )

    return jax.shard_map(
        shards,
        mesh=mesh,
        in_specs=placed,
        out_specs=P("grp", None, None, "gy", None, None, None, None),
        check_vma=False,
    )
```
